32 devices in a mesh: mp: 8 (over z, y), dp: 4 (over x, core).
Axes of the slice: x: 2, y: 2, z: 4, core: 2. Of those that a mesh axis runs over, the one named last changes fastest.
Arguments:
- forward_fields: bfloat16 [16, 4, 16384], P(None, None, 'mp'), may hold values from -6 to 6
- adjoint_fields: bfloat16 [64, 4, 16384], P(None, None, 'mp'), may hold values from -6 to 6
- data_rec: int32 [768], P('dp'), may hold values from 0 to 63
- data_freq: int32 [768], P('dp'), may hold values from 0 to 15
- data_coef: float32 [768, 4], P('dp'), may hold values from -6 to 6
- residual_cols: bfloat16 [768, 256], P('dp'), may hold values from -6 to 6
Outputs:
- data_update: bfloat16 [768, 256], P('dp')
- model_update: float32 [16384, 256], P(('mp', 'dp'))
The draws below stay inside these ranges and needn't reach their ends.
All inputs are finite; a program needn't handle non-finite values.
Results may differ from the reference program's by a relative error of at most 0.0075.
Values may be sent and summed in bfloat16 or wider, within the bound.
A program may use at most 64 MiB of HBM per device.

```python
import math
import jax
import jax.numpy as jnp
from jax import lax

DATA_DEV = 192
GRID_COLS = 128
RHS = 256
NREC = 64
NFREQ = 16
KC = 4
SWEEPS = 2
GRID_ROWS = 128
NCELL = 16384
NDATA = 768


def place_ends(values, stream_key, smallest, largest):
    index_at = [jax.random.randint(jax.random.fold_in(stream_key, axis), (), 0, length) for axis, length in enumerate(values.shape)]
    main_axis = values.shape.index(max(values.shape))
    next_to = index_at[:main_axis] + [(index_at[main_axis] + 1) % values.shape[main_axis]] + index_at[main_axis + 1:]
    return values.at[tuple(index_at)].set(smallest).at[tuple(next_to)].set(largest)


def block_scale(key, shape, split, least, high):
    factor_of, own = 1.0, jax.random.fold_in(key, 6)
    for axis_at, shards_of in split:
        heights = jnp.exp(jax.random.uniform(jax.random.fold_in(own, axis_at), (shards_of,), jnp.float32, least / len(split), high / len(split)))
        factor_of = factor_of * jnp.repeat(heights, shape[axis_at] // shards_of).reshape([-1 if axis == axis_at else 1 for axis in range(len(shape))])
    return factor_of


def scatter_about(own_key, dims, width, reach, split=(), kind=jnp.bfloat16):
    values = jax.random.normal(own_key, dims, jnp.float32) * width
    if len(split) > 0:
        values = block_scale(own_key, dims, split, -0.22, 0.18) * values
    return jnp.clip(values, min=-reach, max=reach).astype(kind)


def setup_inputs(seed: int = 0) -> dict:
    key_of = jax.random.split(jax.random.key(seed), 7)
    return {
        "forward_fields": scatter_about(key_of[0], (NFREQ, KC, NCELL), 1.0, 6.0, ((2, 8),)),
        "adjoint_fields": scatter_about(key_of[1], (NREC, KC, NCELL), 1.0, 6.0, ((2, 8),)),
        "data_rec": place_ends(jax.random.randint(key_of[2], (NDATA,), 0, NREC), jax.random.fold_in(key_of[2], 1), 0, NREC - 1).astype(jnp.int32),
        "data_freq": place_ends(jax.random.randint(key_of[3], (NDATA,), 0, NFREQ), jax.random.fold_in(key_of[3], 1), 0, NFREQ - 1).astype(jnp.int32),
        "data_coef": scatter_about(key_of[4], (NDATA, KC), 1.0, 6.0, ((0, 4),), jnp.float32),
        "residual_cols": scatter_about(key_of[5], (NDATA, RHS), 1.0, 6.0, ((0, 4),)),
    }


def smooth_grid(field):
    for sweep in range(SWEEPS):
        padded = jnp.pad(field, ((0, 0), (1, 1), (1, 1)))
        beside_all = padded[:, :-2, 1:-1] + padded[:, 2:, 1:-1] + padded[:, 1:-1, :-2] + padded[:, 1:-1, 2:]
        field = field + 0.2 * (beside_all - 4.0 * field)
    return field

def reference(forward_fields, adjoint_fields, data_rec, data_freq, data_coef, residual_cols):
    blocks = NDATA // DATA_DEV

    def one_block(index):
        start = index * DATA_DEV
        recs = lax.dynamic_slice_in_dim(data_rec, start, DATA_DEV, 0)
        freqs = lax.dynamic_slice_in_dim(data_freq, start, DATA_DEV, 0)
        coefs = lax.dynamic_slice_in_dim(data_coef, start, DATA_DEV, 0)
        adjoint = adjoint_fields[recs].astype(jnp.float32)
        forward = forward_fields[freqs].astype(jnp.float32)
        sens = (0.5 * lax.optimization_barrier(jnp.sum(coefs[:, :, None] * adjoint * forward, axis=1))).astype(jnp.bfloat16)
        grid = sens.astype(jnp.float32).reshape(DATA_DEV, GRID_ROWS, GRID_COLS)
        smooth = smooth_grid(grid).reshape(DATA_DEV, NCELL).astype(jnp.bfloat16)
        return (sens, smooth)
    sens_all, smooth_all = lax.map(one_block, jnp.arange(blocks, dtype=jnp.int32))
    sens_all = sens_all.reshape(NDATA, NCELL)
    smooth_all = smooth_all.reshape(NDATA, NCELL)
    back = lax.dot_general(sens_all, residual_cols, (((0,), (0,)), ((), ())), preferred_element_type=jnp.float32)
    gram_prod = jnp.dot(smooth_all.astype(jnp.float32), back, precision=lax.Precision.HIGHEST) / NCELL
    data_update = (gram_prod + residual_cols.astype(jnp.float32)).astype(jnp.bfloat16)
    model_update = lax.dot_general(smooth_all, data_update, (((0,), (0,)), ((), ())), preferred_element_type=jnp.float32)
    return (data_update, model_update / math.sqrt(NDATA))
```

```python
import functools
import math

import jax
import jax.numpy as jnp
from jax import lax
from jax.experimental import pallas as pl
from jax.experimental.pallas import tpu as pltpu
from jax.sharding import PartitionSpec as P

COLS = 128
HALO = 2
MESH = pl.DeviceIdType.MESH
F32, BF16 = jnp.float32, jnp.bfloat16


def plan(rows_here, n_mp):
    chunk = 16 * -(-rows_here // (16 * n_mp))
    chunks = rows_here // chunk
    return chunk, chunks, (n_mp - chunks) // 2


def remote(src, dst, send, recv, axis, index):
    return pltpu.make_async_remote_copy(
        src_ref=src, dst_ref=dst, send_sem=send, recv_sem=recv,
        device_id={axis: index}, device_id_type=MESH,
    )


def kernel(
    n_mp, n_dp, ka, kf,
    meta_ref, r_ref, af_ref, du_ref, model_ref,
    meta_all, r_all, win, ohr, ohf, sens, smat, smooth, smooth_t, psend, precv, q, q2, du_all,
    local_sem, halo_send, halo_recv, meta_send, meta_recv, r_send, r_recv,
    s1_send, s1_recv, s2_send, s2_recv, g_send, g_recv, d_send, d_recv,
):
    d, m = lax.axis_index("dp"), lax.axis_index("mp")
    rows_here, rhs = r_ref.shape
    slab = af_ref.shape[1] // COLS
    own = slab // n_dp
    window = own + 2 * HALO
    comps = ohr.shape[0]
    chunk, chunks, first = plan(rows_here, n_mp)
    total_cells = slab * n_mp * COLS

    def dp_peer(t):
        return lax.rem(d + t, n_dp)

    def mp_peer(t):
        return lax.rem(m + t, n_mp)

    def block(index):
        return pl.ds(pl.multiple_of(index * rows_here, 16), rows_here)

    def chunk_of(index, c):
        return pl.ds(pl.multiple_of(index * rows_here + c * chunk, 16), chunk)

    def grid_row(index):
        return pl.ds(pl.multiple_of(index * COLS, COLS), COLS)

    barrier = pltpu.get_barrier_semaphore()
    for t in range(1, n_dp):
        pl.semaphore_signal(barrier, inc=1, device_id={"dp": dp_peer(t)}, device_id_type=MESH)
    for t in range(1, n_mp):
        pl.semaphore_signal(barrier, inc=1, device_id={"mp": mp_peer(t)}, device_id_type=MESH)

    def slab_row(w):
        return d * own - HALO + w

    def in_slab(w):
        return (slab_row(w) >= 0) & (slab_row(w) < slab)

    def local_copy(w):
        return pltpu.make_async_copy(
            af_ref.at[:, grid_row(jnp.clip(slab_row(w), 0, slab - 1))],
            win.at[:, w * COLS:(w + 1) * COLS],
            local_sem.at[w],
        )

    for w in range(window):
        pl.when(in_slab(w))(local_copy(w).start)
    edges = [w for w in range(window) if w < HALO or w >= own + HALO]

    def halo_copy(w):
        step = 1 if w < HALO else -1
        return remote(
            af_ref.at[:, grid_row(jnp.clip(slab_row(w) + step * slab, 0, slab - 1))],
            win.at[:, w * COLS:(w + 1) * COLS],
            halo_send.at[w], halo_recv.at[w], "mp", jnp.clip(m + step, 0, n_mp - 1),
        )

    def halo_sends(w):
        return (slab_row(w) < 0) & (m < n_mp - 1) if w < HALO else (slab_row(w) >= slab) & (m > 0)

    def halo_arrives(w):
        return (slab_row(w) < 0) & (m > 0) if w < HALO else (slab_row(w) >= slab) & (m < n_mp - 1)

    def beyond_grid(w):
        return (slab_row(w) < 0) & (m == 0) if w < HALO else (slab_row(w) >= slab) & (m == n_mp - 1)

    def meta_copy(t):
        return remote(meta_ref, meta_all.at[d], meta_send.at[t], meta_recv.at[d], "dp", dp_peer(t))

    def r_copy(t):
        return remote(r_ref, r_all.at[block(d)], r_send.at[t], r_recv.at[d], "dp", dp_peer(t))

    pl.semaphore_wait(barrier, n_dp + n_mp - 2)
    for t in range(1, n_dp):
        meta_copy(t).start()
    for w in edges:
        pl.when(halo_sends(w))(halo_copy(w).start)
    for t in range(1, n_dp):
        r_copy(t).start()

    meta_all[d] = meta_ref[...]
    r_all[block(d)] = r_ref[...]

    def clear(w):
        win[:, w * COLS:(w + 1) * COLS] = jnp.zeros((ka + 2 * kf, COLS), BF16)

    for w in edges:
        pl.when(beyond_grid(w))(functools.partial(clear, w))

    at = lax.broadcasted_iota(jnp.int32, (COLS, COLS), 0)
    to = lax.broadcasted_iota(jnp.int32, (COLS, COLS), 1)
    apart = jnp.abs(at - to)
    ends = jnp.where(to == 0, 1.0, 0.0) + jnp.where(to == COLS - 1, 1.0, 0.0)
    eye = jnp.where(apart == 0, 1.0, 0.0)
    bands = (
        eye * (5.0 - ends) + jnp.where(apart == 1, 2.0, 0.0) + jnp.where(apart == 2, 1.0, 0.0),
        jnp.where(apart <= 1, 2.0, 0.0),
        eye,
    )
    last_row = slab * n_mp - 1
    for o in range(own):
        row = m * slab + d * own + o
        missing = jnp.where(row == 0, 1.0, 0.0) + jnp.where(row == last_row, 1.0, 0.0)
        for w in range(window):
            gap = abs(w - o - HALO)
            if gap > 2:
                value = jnp.zeros((COLS, COLS), F32)
            else:
                value = bands[gap] - missing * eye if gap == 0 else bands[gap]
            smat[w * COLS:(w + 1) * COLS, o * COLS:(o + 1) * COLS] = value.astype(BF16)

    for t in range(1, n_dp):
        source = dp_peer(t)
        remote(meta_ref, meta_all.at[source], meta_send.at[t], meta_recv.at[source], "dp", source).wait_recv()
    for j in range(n_dp):
        cols = jnp.transpose(meta_all[j])[:rows_here]
        here = slice(j * rows_here, (j + 1) * rows_here)
        ia = lax.broadcasted_iota(jnp.int32, (rows_here, ka), 1).astype(F32)
        jf = lax.broadcasted_iota(jnp.int32, (rows_here, kf), 1).astype(F32)
        for k in range(comps):
            ohr[k, here] = jnp.where(ia == cols[:, 0:1] + float(k), 1.0, 0.0).astype(BF16)
            weight = jnp.where(jf == cols[:, 1:2] + float(k), cols[:, 2 + k:3 + k], 0.0)
            high = weight.astype(BF16)
            ohf[k, here, :kf] = high
            ohf[k, here, kf:] = (weight - high.astype(F32)).astype(BF16)

    wide = 2 if window % 2 == 0 else 1
    tiles = sorted(range(window // wide), key=lambda i: i * wide in edges or i * wide + wide - 1 in edges)
    for i in tiles:
        for w in range(i * wide, (i + 1) * wide):
            pl.when(in_slab(w))(local_copy(w).wait)
            if w in edges:
                pl.when(halo_arrives(w))(halo_copy(w).wait_recv)
        lanes = slice(i * wide * COLS, (i + 1) * wide * COLS)
        for j in range(n_dp):
            here = slice(j * rows_here, (j + 1) * rows_here)
            value = None
            for k in range(comps):
                adjoint = jnp.dot(ohr[k, here], win[:ka, lanes], preferred_element_type=F32)
                forward = jnp.dot(ohf[k, here], win[ka:, lanes], preferred_element_type=F32)
                value = adjoint * forward if value is None else value + adjoint * forward
            sens[here, lanes] = value.astype(BF16)
    smooth[...] = (jnp.dot(sens[...], smat[...], preferred_element_type=F32) * 0.04).astype(BF16)

    for t in range(1, n_dp):
        source = dp_peer(t)
        remote(r_ref, r_all.at[block(source)], r_send.at[t], r_recv.at[source], "dp", source).wait_recv()
    back = lax.dot_general(
        sens[:, HALO * COLS:(HALO + own) * COLS], r_all[...],
        (((0,), (0,)), ((), ())), preferred_element_type=F32,
    ).astype(BF16)

    def p_copy(t):
        return remote(psend.at[t - 1], precv.at[d], s1_send.at[t], s1_recv.at[d], "dp", dp_peer(t))

    for t in range(1, n_dp):
        psend[t - 1] = jnp.dot(smooth[block(dp_peer(t))], back, preferred_element_type=F32).astype(BF16)
        p_copy(t).start()
    total = jnp.dot(smooth[block(d)], back, preferred_element_type=F32)
    smooth_t[...] = jnp.transpose(smooth[...])
    for t in range(1, n_dp):
        source = dp_peer(t)
        remote(psend.at[t - 1], precv.at[source], s1_send.at[t], s1_recv.at[source], "dp", source).wait_recv()
        total = total + precv[source].astype(F32)
    q[...] = total.astype(BF16)

    def q_copy(c):
        return remote(q.at[c * chunk:(c + 1) * chunk], q2.at[m], s2_send.at[c], s2_recv.at[m], "mp", first + c)

    for c in range(chunks):
        pl.when(m != first + c)(q_copy(c).start)
    mine = m - first
    owner = (mine >= 0) & (mine < chunks)
    mine = jnp.clip(mine, 0, chunks - 1)

    def g_copy(t):
        rows = chunk_of(d, mine)
        return remote(du_all.at[rows], du_all.at[rows], g_send.at[t], g_recv.at[mine], "mp", mp_peer(t))

    @pl.when(owner)
    def _():
        q2[m] = q[pl.ds(pl.multiple_of(mine * chunk, 16), chunk)]
        for t in range(1, n_mp):
            source = mp_peer(t)
            remote(q.at[:chunk], q2.at[source], s2_send.at[0], s2_recv.at[source], "mp", source).wait_recv()
        gram = q2[0].astype(F32)
        for i in range(1, n_mp):
            gram = gram + q2[i].astype(F32)
        residual = r_ref[pl.ds(pl.multiple_of(mine * chunk, 16), chunk)].astype(F32)
        du_all[chunk_of(d, mine)] = (gram * (1.0 / total_cells) + residual).astype(BF16)
        for t in range(1, n_mp):
            g_copy(t).start()

    def d_copy(t, c):
        rows = chunk_of(d, c)
        return remote(du_all.at[rows], du_all.at[rows], d_send.at[t, c], d_recv.at[d, c], "dp", dp_peer(t))

    for c in range(chunks):
        rows = chunk_of(d, c)
        arrived = remote(du_all.at[rows], du_all.at[rows], g_send.at[0], g_recv.at[c], "mp", first + c)
        pl.when(m != first + c)(arrived.wait_recv)
        for t in range(1, n_dp):
            d_copy(t, c).start()
    du_ref[...] = du_all[block(d)]
    for t in range(1, n_dp):
        source = dp_peer(t)
        for c in range(chunks):
            rows = chunk_of(source, c)
            remote(du_all.at[rows], du_all.at[rows], d_send.at[t, c], d_recv.at[source, c], "dp", source).wait_recv()
    model_ref[...] = jnp.dot(smooth_t[...], du_all[...], preferred_element_type=F32) * (
        1.0 / math.sqrt(rows_here * n_dp)
    )

    for w in edges:
        pl.when(halo_sends(w))(halo_copy(w).wait_send)
    for t in range(1, n_dp):
        meta_copy(t).wait_send()
        r_copy(t).wait_send()
        p_copy(t).wait_send()
        for c in range(chunks):
            d_copy(t, c).wait_send()
    for c in range(chunks):
        pl.when(m != first + c)(q_copy(c).wait_send)

    @pl.when(owner)
    def _():
        for t in range(1, n_mp):
            g_copy(t).wait_send()


def per_device(n_mp, n_dp, forward_fields, adjoint_fields, data_rec, data_freq, data_coef, residual_cols):
    rows_here, rhs = residual_cols.shape
    cells = forward_fields.shape[2]
    comps = forward_fields.shape[1]
    ka, kf = adjoint_fields.shape[0] * comps, forward_fields.shape[0] * comps
    data = rows_here * n_dp
    own = cells // COLS // n_dp
    window = own + 2 * HALO
    chunk, chunks, first = plan(rows_here, n_mp)
    forward = forward_fields.reshape(kf, cells)
    af = jnp.concatenate([adjoint_fields.reshape(ka, cells), forward, forward], axis=0)
    meta = jnp.concatenate(
        [(data_rec * comps)[None].astype(F32), (data_freq * comps)[None].astype(F32), 0.5 * data_coef.T],
        axis=0,
    )
    meta = jnp.pad(meta, ((0, 8 - meta.shape[0]), (0, -rows_here % 128)))
    dma = pltpu.SemaphoreType.DMA
    vmem = pl.BlockSpec(memory_space=pltpu.VMEM)
    return pl.pallas_call(
        functools.partial(kernel, n_mp, n_dp, ka, kf),
        out_shape=(
            jax.ShapeDtypeStruct((rows_here, rhs), BF16),
            jax.ShapeDtypeStruct((own * COLS, rhs), F32),
        ),
        in_specs=[vmem, vmem, pl.BlockSpec(memory_space=pl.ANY)],
        out_specs=(vmem, vmem),
        scratch_shapes=[
            pltpu.VMEM((n_dp,) + meta.shape, F32),
            pltpu.VMEM((data, rhs), BF16),
            pltpu.VMEM((ka + 2 * kf, window * COLS), BF16),
            pltpu.VMEM((comps, data, ka), BF16),
            pltpu.VMEM((comps, data, 2 * kf), BF16),
            pltpu.VMEM((data, window * COLS), BF16),
            pltpu.VMEM((window * COLS, own * COLS), BF16),
            pltpu.VMEM((data, own * COLS), BF16),
            pltpu.VMEM((own * COLS, data), BF16),
            pltpu.VMEM((n_dp - 1, rows_here, rhs), BF16),
            pltpu.VMEM((n_dp, rows_here, rhs), BF16),
            pltpu.VMEM((rows_here, rhs), BF16),
            pltpu.VMEM((n_mp, chunk, rhs), BF16),
            pltpu.VMEM((data, rhs), BF16),
            dma((window,)), dma((window,)), dma((window,)),
            dma((n_dp,)), dma((n_dp,)), dma((n_dp,)), dma((n_dp,)),
            dma((n_dp,)), dma((n_dp,)),
            dma((chunks,)), dma((n_mp,)),
            dma((n_mp,)), dma((chunks,)),
            dma((n_dp, chunks)), dma((n_dp, chunks)),
        ],
        compiler_params=pltpu.CompilerParams(collective_id=0, has_side_effects=True, vmem_limit_bytes=60 * 1024 * 1024),
    )(meta, residual_cols, af)


def solution(mesh):
    in_specs = (
        P(None, None, "mp"),
        P(None, None, "mp"),
        P("dp"),
        P("dp"),
        P("dp", None),
        P("dp", None),
    )
    out_specs = (P("dp", None), P(("mp", "dp"), None))
    body = functools.partial(per_device, mesh.shape["mp"], mesh.shape["dp"])
    return jax.shard_map(body, mesh=mesh, in_specs=in_specs, out_specs=out_specs, check_vma=False)
```

```python
import functools
import math

import jax
import jax.numpy as jnp
from jax import lax
from jax.experimental import pallas as pl
from jax.experimental.pallas import tpu as pltpu
from jax.sharding import PartitionSpec as P

COLS = 128
HALO = 2
MESH = pl.DeviceIdType.MESH
F32, BF16 = jnp.float32, jnp.bfloat16


def plan(rows_here, n_mp):
    chunk = 16 * -(-rows_here // (16 * n_mp))
    chunks = rows_here // chunk
    return chunk, chunks, (n_mp - chunks) // 2


def remote(src, dst, send, recv, axis, index):
    return pltpu.make_async_remote_copy(
        src_ref=src, dst_ref=dst, send_sem=send, recv_sem=recv,
        device_id={axis: index}, device_id_type=MESH,
    )


def kernel(
    n_mp, n_dp, ka, kf,
    rec_ref, freq_ref, coef_ref, r_ref, a_ref, f_ref, du_all, smooth_t,
    meta, meta_all, r_all, win, ohr, ohf, sens, smat, smooth, psend, precv, q, q2,
    local_sem, halo_send, halo_recv, meta_send, meta_recv, r_send, r_recv,
    s1_send, s1_recv, s2_send, s2_recv, g_send, g_recv, d_send, d_recv,
):
    d, m = lax.axis_index("dp"), lax.axis_index("mp")
    rows_here, rhs = r_ref.shape
    slab = a_ref.shape[1] // COLS
    own = slab // n_dp
    window = own + 2 * HALO
    comps = ohr.shape[0]
    chunk, chunks, first = plan(rows_here, n_mp)
    total_cells = slab * n_mp * COLS

    def dp_peer(t):
        return lax.rem(d + t, n_dp)

    def mp_peer(t):
        return lax.rem(m + t, n_mp)

    def block(index):
        return pl.ds(pl.multiple_of(index * rows_here, 16), rows_here)

    def chunk_of(index, c):
        return pl.ds(pl.multiple_of(index * rows_here + c * chunk, 16), chunk)

    def grid_row(index):
        return pl.ds(pl.multiple_of(index * COLS, COLS), COLS)

    barrier = pltpu.get_barrier_semaphore()
    for t in range(1, n_dp):
        pl.semaphore_signal(barrier, inc=1, device_id={"dp": dp_peer(t)}, device_id_type=MESH)
    for t in range(1, n_mp):
        pl.semaphore_signal(barrier, inc=1, device_id={"mp": mp_peer(t)}, device_id_type=MESH)

    def slab_row(w):
        return d * own - HALO + w

    def in_slab(w):
        return (slab_row(w) >= 0) & (slab_row(w) < slab)

    halves = ((a_ref, slice(0, ka)), (f_ref, slice(ka, ka + kf)))

    def start_all(copies):
        for copy in copies:
            copy.start()

    def wait_all(copies):
        for copy in copies:
            copy.wait()

    def wait_recv_all(copies):
        for copy in copies:
            copy.wait_recv()

    def wait_send_all(copies):
        for copy in copies:
            copy.wait_send()

    def local_copy(w):
        row = grid_row(jnp.clip(slab_row(w), 0, slab - 1))
        return [
            pltpu.make_async_copy(ref.at[:, row], win.at[part, w * COLS:(w + 1) * COLS], local_sem.at[h, w])
            for h, (ref, part) in enumerate(halves)
        ]

    for w in range(window):
        pl.when(in_slab(w))(lambda w=w: start_all(local_copy(w)))
    edges = [w for w in range(window) if w < HALO or w >= own + HALO]

    def halo_copy(w):
        step = 1 if w < HALO else -1
        row = grid_row(jnp.clip(slab_row(w) + step * slab, 0, slab - 1))
        return [
            remote(
                ref.at[:, row], win.at[part, w * COLS:(w + 1) * COLS],
                halo_send.at[h, w], halo_recv.at[h, w], "mp", jnp.clip(m + step, 0, n_mp - 1),
            )
            for h, (ref, part) in enumerate(halves)
        ]

    def halo_sends(w):
        return (slab_row(w) < 0) & (m < n_mp - 1) if w < HALO else (slab_row(w) >= slab) & (m > 0)

    def halo_arrives(w):
        return (slab_row(w) < 0) & (m > 0) if w < HALO else (slab_row(w) >= slab) & (m < n_mp - 1)

    def beyond_grid(w):
        return (slab_row(w) < 0) & (m == 0) if w < HALO else (slab_row(w) >= slab) & (m == n_mp - 1)

    def meta_copy(t):
        return remote(meta, meta_all.at[d], meta_send.at[t], meta_recv.at[d], "dp", dp_peer(t))

    def r_copy(t):
        return remote(r_ref, r_all.at[block(d)], r_send.at[t], r_recv.at[d], "dp", dp_peer(t))

    meta[...] = jnp.zeros_like(meta)
    meta[0:1, :rows_here] = rec_ref[...].astype(F32) * float(comps)
    meta[1:2, :rows_here] = freq_ref[...].astype(F32) * float(comps)
    meta[2:2 + comps, :rows_here] = 0.5 * coef_ref[...]

    at = lax.broadcasted_iota(jnp.int32, (COLS, COLS), 0)
    to = lax.broadcasted_iota(jnp.int32, (COLS, COLS), 1)
    apart = jnp.abs(at - to)
    ends = jnp.where(to == 0, 1.0, 0.0) + jnp.where(to == COLS - 1, 1.0, 0.0)
    eye = jnp.where(apart == 0, 1.0, 0.0)
    bands = (
        eye * (5.0 - ends) + jnp.where(apart == 1, 2.0, 0.0) + jnp.where(apart == 2, 1.0, 0.0),
        jnp.where(apart <= 1, 2.0, 0.0),
        eye,
    )
    last_row = slab * n_mp - 1
    for o in range(own):
        row = m * slab + d * own + o
        missing = jnp.where(row == 0, 1.0, 0.0) + jnp.where(row == last_row, 1.0, 0.0)
        for w in range(window):
            gap = abs(w - o - HALO)
            if gap > 2:
                value = jnp.zeros((COLS, COLS), F32)
            else:
                value = bands[gap] - missing * eye if gap == 0 else bands[gap]
            smat[w * COLS:(w + 1) * COLS, o * COLS:(o + 1) * COLS] = value.astype(BF16)

    pl.semaphore_wait(barrier, n_dp + n_mp - 2)
    for t in range(1, n_dp):
        meta_copy(t).start()
    for w in edges:
        pl.when(halo_sends(w))(lambda w=w: start_all(halo_copy(w)))
    for t in range(1, n_dp):
        r_copy(t).start()

    meta_all[d] = meta[...]
    r_all[block(d)] = r_ref[...]

    def clear(w):
        win[:, w * COLS:(w + 1) * COLS] = jnp.zeros((ka + 2 * kf, COLS), BF16)

    for w in edges:
        pl.when(beyond_grid(w))(functools.partial(clear, w))

    def select(j):
        cols = jnp.transpose(meta_all[j])[:rows_here]
        here = block(j)
        ia = lax.broadcasted_iota(jnp.int32, (rows_here, ka), 1).astype(F32)
        jf = lax.broadcasted_iota(jnp.int32, (rows_here, kf), 1).astype(F32)
        for k in range(comps):
            ohr[k, here] = jnp.where(ia == cols[:, 0:1] + float(k), 1.0, 0.0).astype(BF16)
            weight = jnp.where(jf == cols[:, 1:2] + float(k), cols[:, 2 + k:3 + k], 0.0)
            high = weight.astype(BF16)
            low = (weight - high.astype(F32)).astype(BF16)
            ohf[k, here] = jnp.concatenate([high, low], axis=1)

    wide = 2 if window % 2 == 0 else 1
    tiles = range(window // wide)
    edge_tiles = [i for i in tiles if any(i * wide + b in edges for b in range(wide))]
    inner_tiles = [i for i in tiles if i not in edge_tiles]

    def fields_ready(i):
        for w in range(i * wide, (i + 1) * wide):
            pl.when(in_slab(w))(lambda w=w: wait_all(local_copy(w)))
            if w in edges:
                pl.when(halo_arrives(w))(lambda w=w: wait_recv_all(halo_copy(w)))
        lanes = slice(i * wide * COLS, (i + 1) * wide * COLS)
        win[ka + kf:, lanes] = win[ka:ka + kf, lanes]

    def make_sens(i, j):
        lanes = slice(i * wide * COLS, (i + 1) * wide * COLS)
        here = block(j)
        value = None
        for k in range(comps):
            adjoint = jnp.dot(ohr[k, here], win[:ka, lanes], preferred_element_type=F32)
            forward = jnp.dot(ohf[k, here], win[ka:, lanes], preferred_element_type=F32)
            value = adjoint * forward if value is None else value + adjoint * forward
        sens[here, lanes] = value.astype(BF16)

    select(d)
    for i in inner_tiles:
        fields_ready(i)
        make_sens(i, d)
    for t in range(1, n_dp):
        source = dp_peer(t)
        remote(meta, meta_all.at[source], meta_send.at[t], meta_recv.at[source], "dp", source).wait_recv()
        select(source)
        for i in inner_tiles:
            make_sens(i, source)
    for i in edge_tiles:
        fields_ready(i)
        for j in range(n_dp):
            make_sens(i, j)
    smooth[...] = (jnp.dot(sens[...], smat[...], preferred_element_type=F32) * 0.04).astype(BF16)

    for t in range(1, n_dp):
        source = dp_peer(t)
        remote(r_ref, r_all.at[block(source)], r_send.at[t], r_recv.at[source], "dp", source).wait_recv()
    back = lax.dot_general(
        sens[:, HALO * COLS:(HALO + own) * COLS], r_all[...],
        (((0,), (0,)), ((), ())), preferred_element_type=F32,
    ).astype(BF16)

    def p_copy(t):
        return remote(psend.at[t - 1], precv.at[d], s1_send.at[t], s1_recv.at[d], "dp", dp_peer(t))

    for t in range(1, n_dp):
        psend[t - 1] = jnp.dot(smooth[block(dp_peer(t))], back, preferred_element_type=F32).astype(BF16)
        p_copy(t).start()
    total = jnp.dot(smooth[block(d)], back, preferred_element_type=F32)
    smooth_t[...] = jnp.transpose(smooth[...])
    for t in range(1, n_dp):
        source = dp_peer(t)
        remote(psend.at[t - 1], precv.at[source], s1_send.at[t], s1_recv.at[source], "dp", source).wait_recv()
        total = total + precv[source].astype(F32)
    q[...] = total.astype(BF16)

    def q_copy(c):
        return remote(q.at[c * chunk:(c + 1) * chunk], q2.at[m], s2_send.at[c], s2_recv.at[m], "mp", first + c)

    for c in range(chunks):
        pl.when(m != first + c)(q_copy(c).start)
    mine = m - first
    owner = (mine >= 0) & (mine < chunks)
    mine = jnp.clip(mine, 0, chunks - 1)

    def g_copy(t):
        rows = chunk_of(d, mine)
        return remote(du_all.at[rows], du_all.at[rows], g_send.at[t], g_recv.at[mine], "mp", mp_peer(t))

    @pl.when(owner)
    def _():
        q2[m] = q[pl.ds(pl.multiple_of(mine * chunk, 16), chunk)]
        for t in range(1, n_mp):
            source = mp_peer(t)
            remote(q.at[:chunk], q2.at[source], s2_send.at[0], s2_recv.at[source], "mp", source).wait_recv()
        gram = q2[0].astype(F32)
        for i in range(1, n_mp):
            gram = gram + q2[i].astype(F32)
        residual = r_ref[pl.ds(pl.multiple_of(mine * chunk, 16), chunk)].astype(F32)
        du_all[chunk_of(d, mine)] = (gram * (1.0 / total_cells) + residual).astype(BF16)
        for t in range(1, n_mp):
            g_copy(t).start()

    far = [2 * s for s in range(1, n_dp // 2)]
    partner = d + 1 - 2 * lax.rem(d, 2)

    def d_copy(slot, source, c, to):
        rows = chunk_of(source, c)
        return remote(du_all.at[rows], du_all.at[rows], d_send.at[slot, c], d_recv.at[source, c], "dp", to)

    def own_copies(c):
        return [d_copy(s, d, c, dp_peer(t)) for s, t in enumerate(far)] + [d_copy(len(far), d, c, partner)]

    def relay(s, c):
        return d_copy(len(far) + 1 + s, dp_peer(far[s]), c, partner)

    for c in range(chunks):
        rows = chunk_of(d, c)
        arrived = remote(du_all.at[rows], du_all.at[rows], g_send.at[0], g_recv.at[c], "mp", first + c)
        pl.when(m != first + c)(arrived.wait_recv)
        start_all(own_copies(c))
    for c in range(chunks):
        for s, t in enumerate(far):
            d_copy(0, dp_peer(t), c, dp_peer(t)).wait_recv()
            relay(s, c).start()
    for c in range(chunks):
        d_copy(0, partner, c, partner).wait_recv()
        for s, t in enumerate(far):
            d_copy(0, lax.rem(partner + t, n_dp), c, partner).wait_recv()

    for w in edges:
        pl.when(halo_sends(w))(lambda w=w: wait_send_all(halo_copy(w)))
    for t in range(1, n_dp):
        meta_copy(t).wait_send()
        r_copy(t).wait_send()
        p_copy(t).wait_send()
    for c in range(chunks):
        pl.when(m != first + c)(q_copy(c).wait_send)
        wait_send_all(own_copies(c))
        for s in range(len(far)):
            relay(s, c).wait_send()

    @pl.when(owner)
    def _():
        for t in range(1, n_mp):
            g_copy(t).wait_send()


def finish(n_dp, smooth_t, du_all, du_ref, model_ref):
    rows_here = du_ref.shape[0]
    d = lax.axis_index("dp")
    du_ref[...] = du_all[pl.ds(pl.multiple_of(d * rows_here, 16), rows_here)]
    model_ref[...] = jnp.dot(smooth_t[...], du_all[...], preferred_element_type=F32) * (
        1.0 / math.sqrt(rows_here * n_dp)
    )


def per_device(n_mp, n_dp, forward_fields, adjoint_fields, data_rec, data_freq, data_coef, residual_cols):
    rows_here, rhs = residual_cols.shape
    cells = forward_fields.shape[2]
    comps = forward_fields.shape[1]
    ka, kf = adjoint_fields.shape[0] * comps, forward_fields.shape[0] * comps
    data = rows_here * n_dp
    own = cells // COLS // n_dp
    window = own + 2 * HALO
    chunk, chunks, first = plan(rows_here, n_mp)
    meta_shape = (8, rows_here + -rows_here % 128)
    dma = pltpu.SemaphoreType.DMA
    vmem = pl.BlockSpec(memory_space=pltpu.VMEM)
    du_all, smooth_t = pl.pallas_call(
        functools.partial(kernel, n_mp, n_dp, ka, kf),
        out_shape=(
            jax.ShapeDtypeStruct((data, rhs), BF16),
            jax.ShapeDtypeStruct((own * COLS, data), BF16),
        ),
        in_specs=[vmem] * 4 + [pl.BlockSpec(memory_space=pl.ANY)] * 2,
        out_specs=(vmem, vmem),
        scratch_shapes=[
            pltpu.VMEM(meta_shape, F32),
            pltpu.VMEM((n_dp,) + meta_shape, F32),
            pltpu.VMEM((data, rhs), BF16),
            pltpu.VMEM((ka + 2 * kf, window * COLS), BF16),
            pltpu.VMEM((comps, data, ka), BF16),
            pltpu.VMEM((comps, data, 2 * kf), BF16),
            pltpu.VMEM((data, window * COLS), BF16),
            pltpu.VMEM((window * COLS, own * COLS), BF16),
            pltpu.VMEM((data, own * COLS), BF16),
            pltpu.VMEM((n_dp - 1, rows_here, rhs), BF16),
            pltpu.VMEM((n_dp, rows_here, rhs), BF16),
            pltpu.VMEM((rows_here, rhs), BF16),
            pltpu.VMEM((n_mp, chunk, rhs), BF16),
            dma((2, window)), dma((2, window)), dma((2, window)),
            dma((n_dp,)), dma((n_dp,)), dma((n_dp,)), dma((n_dp,)),
            dma((n_dp,)), dma((n_dp,)),
            dma((chunks,)), dma((n_mp,)),
            dma((n_mp,)), dma((chunks,)),
            dma((n_dp, chunks)), dma((n_dp, chunks)),
        ],
        compiler_params=pltpu.CompilerParams(
            collective_id=0, has_side_effects=True, vmem_limit_bytes=44 * 1024 * 1024
        ),
    )(
        data_rec[None], data_freq[None], data_coef.T, residual_cols,
        adjoint_fields.reshape(ka, cells), forward_fields.reshape(kf, cells),
    )
    return pl.pallas_call(
        functools.partial(finish, n_dp),
        out_shape=(
            jax.ShapeDtypeStruct((rows_here, rhs), BF16),
            jax.ShapeDtypeStruct((own * COLS, rhs), F32),
        ),
        in_specs=[vmem, vmem],
        out_specs=(vmem, vmem),
        compiler_params=pltpu.CompilerParams(vmem_limit_bytes=16 * 1024 * 1024),
    )(smooth_t, du_all)


def solution(mesh):
    in_specs = (
        P(None, None, "mp"),
        P(None, None, "mp"),
        P("dp"),
        P("dp"),
        P("dp", None),
        P("dp", None),
    )
    out_specs = (P("dp", None), P(("mp", "dp"), None))
    body = functools.partial(per_device, mesh.shape["mp"], mesh.shape["dp"])
    return jax.shard_map(body, mesh=mesh, in_specs=in_specs, out_specs=out_specs, check_vma=False)
```

```python
import functools
import math

import jax
import jax.numpy as jnp
from jax import lax
from jax.experimental import pallas as pl
from jax.experimental.pallas import tpu as pltpu
from jax.sharding import PartitionSpec as P

COLS = 128
HALO = 2
MESH = pl.DeviceIdType.MESH
F32, BF16 = jnp.float32, jnp.bfloat16


def plan(rows_here, n_mp):
    chunk = 16 * -(-rows_here // (16 * n_mp))
    chunks = rows_here // chunk
    return chunk, chunks, (n_mp - chunks) // 2


def remote(src, dst, send, recv, axis, index):
    return pltpu.make_async_remote_copy(
        src_ref=src, dst_ref=dst, send_sem=send, recv_sem=recv,
        device_id={axis: index}, device_id_type=MESH,
    )


def kernel(
    n_mp, n_dp, ka, kf,
    rec_ref, freq_ref, coef_ref, r_ref, a_ref, f_ref, du_all, smooth_t,
    meta, meta_all, r_all, win, ohr, ohf, sens, smat, smooth, psend, precv, q, q2,
    local_sem, halo_send, halo_recv, meta_send, meta_recv, r_send, r_recv,
    s1_send, s1_recv, s2_send, s2_recv, g_send, g_recv, d_send, d_recv,
):
    d, m = lax.axis_index("dp"), lax.axis_index("mp")
    rows_here, rhs = r_ref.shape
    slab = a_ref.shape[1] // COLS
    own = slab // n_dp
    window = own + 2 * HALO
    comps = ohr.shape[0]
    chunk, chunks, first = plan(rows_here, n_mp)
    total_cells = slab * n_mp * COLS

    def dp_peer(t):
        return lax.rem(d + t, n_dp)

    def mp_peer(t):
        return lax.rem(m + t, n_mp)

    def block(index):
        return pl.ds(pl.multiple_of(index * rows_here, 16), rows_here)

    def chunk_of(index, c):
        return pl.ds(pl.multiple_of(index * rows_here + c * chunk, 16), chunk)

    def grid_row(index):
        return pl.ds(pl.multiple_of(index * COLS, COLS), COLS)

    barrier = pltpu.get_barrier_semaphore()
    for t in range(1, n_dp):
        pl.semaphore_signal(barrier, inc=1, device_id={"dp": dp_peer(t)}, device_id_type=MESH)
    for t in range(1, n_mp):
        pl.semaphore_signal(barrier, inc=1, device_id={"mp": mp_peer(t)}, device_id_type=MESH)

    def slab_row(w):
        return d * own - HALO + w

    def in_slab(w):
        return (slab_row(w) >= 0) & (slab_row(w) < slab)

    halves = ((a_ref, slice(0, ka)), (f_ref, slice(ka, ka + kf)))

    def start_all(copies):
        for copy in copies:
            copy.start()

    def wait_all(copies):
        for copy in copies:
            copy.wait()

    def wait_recv_all(copies):
        for copy in copies:
            copy.wait_recv()

    def wait_send_all(copies):
        for copy in copies:
            copy.wait_send()

    def local_copy(w):
        row = grid_row(jnp.clip(slab_row(w), 0, slab - 1))
        return [
            pltpu.make_async_copy(ref.at[:, row], win.at[part, w * COLS:(w + 1) * COLS], local_sem.at[h, w])
            for h, (ref, part) in enumerate(halves)
        ]

    for w in range(window):
        pl.when(in_slab(w))(lambda w=w: start_all(local_copy(w)))
    edges = [w for w in range(window) if w < HALO or w >= own + HALO]

    def halo_copy(w):
        step = 1 if w < HALO else -1
        row = grid_row(jnp.clip(slab_row(w) + step * slab, 0, slab - 1))
        return [
            remote(
                ref.at[:, row], win.at[part, w * COLS:(w + 1) * COLS],
                halo_send.at[h, w], halo_recv.at[h, w], "mp", jnp.clip(m + step, 0, n_mp - 1),
            )
            for h, (ref, part) in enumerate(halves)
        ]

    def halo_sends(w):
        return (slab_row(w) < 0) & (m < n_mp - 1) if w < HALO else (slab_row(w) >= slab) & (m > 0)

    def halo_arrives(w):
        return (slab_row(w) < 0) & (m > 0) if w < HALO else (slab_row(w) >= slab) & (m < n_mp - 1)

    def beyond_grid(w):
        return (slab_row(w) < 0) & (m == 0) if w < HALO else (slab_row(w) >= slab) & (m == n_mp - 1)

    def meta_copy(t):
        return remote(meta, meta_all.at[d], meta_send.at[t], meta_recv.at[d], "dp", dp_peer(t))

    def r_copy(t):
        return remote(r_ref, r_all.at[block(d)], r_send.at[t], r_recv.at[d], "dp", dp_peer(t))

    meta[...] = jnp.zeros_like(meta)
    meta[0:1, :rows_here] = rec_ref[...].astype(F32) * float(comps)
    meta[1:2, :rows_here] = freq_ref[...].astype(F32) * float(comps)
    meta[2:2 + comps, :rows_here] = 0.5 * coef_ref[...]

    at = lax.broadcasted_iota(jnp.int32, (COLS, COLS), 0)
    to = lax.broadcasted_iota(jnp.int32, (COLS, COLS), 1)
    apart = jnp.abs(at - to)
    ends = jnp.where(to == 0, 1.0, 0.0) + jnp.where(to == COLS - 1, 1.0, 0.0)
    eye = jnp.where(apart == 0, 1.0, 0.0)
    bands = (
        eye * (5.0 - ends) + jnp.where(apart == 1, 2.0, 0.0) + jnp.where(apart == 2, 1.0, 0.0),
        jnp.where(apart <= 1, 2.0, 0.0),
        eye,
    )
    last_row = slab * n_mp - 1
    for o in range(own):
        row = m * slab + d * own + o
        missing = jnp.where(row == 0, 1.0, 0.0) + jnp.where(row == last_row, 1.0, 0.0)
        for w in range(window):
            gap = abs(w - o - HALO)
            if gap > 2:
                value = jnp.zeros((COLS, COLS), F32)
            else:
                value = bands[gap] - missing * eye if gap == 0 else bands[gap]
            smat[w * COLS:(w + 1) * COLS, o * COLS:(o + 1) * COLS] = value.astype(BF16)

    meta_all[d] = meta[...]

    def select(j):
        cols = jnp.transpose(meta_all[j])[:rows_here]
        here = block(j)
        ia = lax.broadcasted_iota(jnp.int32, (rows_here, ka), 1).astype(F32)
        jf = lax.broadcasted_iota(jnp.int32, (rows_here, kf), 1).astype(F32)
        for k in range(comps):
            ohr[k, here] = jnp.where(ia == cols[:, 0:1] + float(k), 1.0, 0.0).astype(BF16)
            weight = jnp.where(jf == cols[:, 1:2] + float(k), cols[:, 2 + k:3 + k], 0.0)
            high = weight.astype(BF16)
            low = (weight - high.astype(F32)).astype(BF16)
            ohf[k, here] = jnp.concatenate([high, low], axis=1)

    select(d)
    pl.semaphore_wait(barrier, n_dp + n_mp - 2)
    for t in range(1, n_dp):
        meta_copy(t).start()
    for w in edges:
        pl.when(halo_sends(w))(lambda w=w: start_all(halo_copy(w)))
    for t in range(1, n_dp):
        r_copy(t).start()

    r_all[block(d)] = r_ref[...]

    def clear(w):
        win[:, w * COLS:(w + 1) * COLS] = jnp.zeros((ka + 2 * kf, COLS), BF16)

    for w in edges:
        pl.when(beyond_grid(w))(functools.partial(clear, w))

    wide = 2 if window % 2 == 0 else 1
    tiles = range(window // wide)
    edge_tiles = [i for i in tiles if any(i * wide + b in edges for b in range(wide))]
    inner_tiles = [i for i in tiles if i not in edge_tiles]

    def fields_ready(i):
        for w in range(i * wide, (i + 1) * wide):
            pl.when(in_slab(w))(lambda w=w: wait_all(local_copy(w)))
            if w in edges:
                pl.when(halo_arrives(w))(lambda w=w: wait_recv_all(halo_copy(w)))
        lanes = slice(i * wide * COLS, (i + 1) * wide * COLS)
        win[ka + kf:, lanes] = win[ka:ka + kf, lanes]

    def make_sens(i, j):
        lanes = slice(i * wide * COLS, (i + 1) * wide * COLS)
        here = block(j)
        value = None
        for k in range(comps):
            adjoint = jnp.dot(ohr[k, here], win[:ka, lanes], preferred_element_type=F32)
            forward = jnp.dot(ohf[k, here], win[ka:, lanes], preferred_element_type=F32)
            value = adjoint * forward if value is None else value + adjoint * forward
        sens[here, lanes] = value.astype(BF16)

    for i in inner_tiles:
        fields_ready(i)
        make_sens(i, d)
    for t in range(1, n_dp):
        source = dp_peer(t)
        remote(meta, meta_all.at[source], meta_send.at[t], meta_recv.at[source], "dp", source).wait_recv()
        select(source)
        for i in inner_tiles:
            make_sens(i, source)
    for i in edge_tiles:
        fields_ready(i)
        for j in range(n_dp):
            make_sens(i, j)
    smooth[...] = (jnp.dot(sens[...], smat[...], preferred_element_type=F32) * 0.04).astype(BF16)

    for t in range(1, n_dp):
        source = dp_peer(t)
        remote(r_ref, r_all.at[block(source)], r_send.at[t], r_recv.at[source], "dp", source).wait_recv()
    back = lax.dot_general(
        sens[:, HALO * COLS:(HALO + own) * COLS], r_all[...],
        (((0,), (0,)), ((), ())), preferred_element_type=F32,
    ).astype(BF16)

    def p_copy(t):
        return remote(psend.at[t - 1], precv.at[d], s1_send.at[t], s1_recv.at[d], "dp", dp_peer(t))

    for t in range(1, n_dp):
        psend[t - 1] = jnp.dot(smooth[block(dp_peer(t))], back, preferred_element_type=F32).astype(BF16)
        p_copy(t).start()
    total = jnp.dot(smooth[block(d)], back, preferred_element_type=F32)
    smooth_t[...] = jnp.transpose(smooth[...])
    for t in range(1, n_dp):
        source = dp_peer(t)
        remote(psend.at[t - 1], precv.at[source], s1_send.at[t], s1_recv.at[source], "dp", source).wait_recv()
        total = total + precv[source].astype(F32)
    q[...] = total.astype(BF16)

    def q_copy(c):
        return remote(q.at[c * chunk:(c + 1) * chunk], q2.at[m], s2_send.at[c], s2_recv.at[m], "mp", first + c)

    for c in range(chunks):
        pl.when(m != first + c)(q_copy(c).start)
    mine = m - first
    owner = (mine >= 0) & (mine < chunks)
    mine = jnp.clip(mine, 0, chunks - 1)

    def g_copy(t):
        rows = chunk_of(d, mine)
        return remote(du_all.at[rows], du_all.at[rows], g_send.at[t], g_recv.at[mine], "mp", mp_peer(t))

    @pl.when(owner)
    def _():
        q2[m] = q[pl.ds(pl.multiple_of(mine * chunk, 16), chunk)]
        for t in range(1, n_mp):
            source = mp_peer(t)
            remote(q.at[:chunk], q2.at[source], s2_send.at[0], s2_recv.at[source], "mp", source).wait_recv()
        gram = q2[0].astype(F32)
        for i in range(1, n_mp):
            gram = gram + q2[i].astype(F32)
        residual = r_ref[pl.ds(pl.multiple_of(mine * chunk, 16), chunk)].astype(F32)
        du_all[chunk_of(d, mine)] = (gram * (1.0 / total_cells) + residual).astype(BF16)
        for t in range(1, n_mp):
            g_copy(t).start()

    far = [2 * s for s in range(1, n_dp // 2)]
    partner = d + 1 - 2 * lax.rem(d, 2)

    def d_copy(slot, source, c, to):
        rows = chunk_of(source, c)
        return remote(du_all.at[rows], du_all.at[rows], d_send.at[slot, c], d_recv.at[source, c], "dp", to)

    def own_copies(c):
        return [d_copy(s, d, c, dp_peer(t)) for s, t in enumerate(far)] + [d_copy(len(far), d, c, partner)]

    def relay(s, c):
        return d_copy(len(far) + 1 + s, dp_peer(far[s]), c, partner)

    for c in range(chunks):
        rows = chunk_of(d, c)
        arrived = remote(du_all.at[rows], du_all.at[rows], g_send.at[0], g_recv.at[c], "mp", first + c)
        pl.when(m != first + c)(arrived.wait_recv)
        start_all(own_copies(c))
    for c in range(chunks):
        for s, t in enumerate(far):
            d_copy(0, dp_peer(t), c, dp_peer(t)).wait_recv()
            relay(s, c).start()
    for c in range(chunks):
        d_copy(0, partner, c, partner).wait_recv()
        for s, t in enumerate(far):
            d_copy(0, lax.rem(partner + t, n_dp), c, partner).wait_recv()

    for w in edges:
        pl.when(halo_sends(w))(lambda w=w: wait_send_all(halo_copy(w)))
    for t in range(1, n_dp):
        meta_copy(t).wait_send()
        r_copy(t).wait_send()
        p_copy(t).wait_send()
    for c in range(chunks):
        pl.when(m != first + c)(q_copy(c).wait_send)
        wait_send_all(own_copies(c))
        for s in range(len(far)):
            relay(s, c).wait_send()

    @pl.when(owner)
    def _():
        for t in range(1, n_mp):
            g_copy(t).wait_send()


def finish(n_dp, smooth_t, du_all, du_ref, model_ref):
    rows_here = du_ref.shape[0]
    d = lax.axis_index("dp")
    du_ref[...] = du_all[pl.ds(pl.multiple_of(d * rows_here, 16), rows_here)]
    model_ref[...] = jnp.dot(smooth_t[...], du_all[...], preferred_element_type=F32) * (
        1.0 / math.sqrt(rows_here * n_dp)
    )


def per_device(n_mp, n_dp, forward_fields, adjoint_fields, data_rec, data_freq, data_coef, residual_cols):
    rows_here, rhs = residual_cols.shape
    cells = forward_fields.shape[2]
    comps = forward_fields.shape[1]
    ka, kf = adjoint_fields.shape[0] * comps, forward_fields.shape[0] * comps
    data = rows_here * n_dp
    own = cells // COLS // n_dp
    window = own + 2 * HALO
    chunk, chunks, first = plan(rows_here, n_mp)
    meta_shape = (8, rows_here + -rows_here % 128)
    adjoint, forward = lax.optimization_barrier((adjoint_fields.reshape(ka, cells), forward_fields))
    dma = pltpu.SemaphoreType.DMA
    vmem = pl.BlockSpec(memory_space=pltpu.VMEM)
    du_all, smooth_t = pl.pallas_call(
        functools.partial(kernel, n_mp, n_dp, ka, kf),
        out_shape=(
            jax.ShapeDtypeStruct((data, rhs), BF16),
            jax.ShapeDtypeStruct((own * COLS, data), BF16),
        ),
        in_specs=[vmem] * 4 + [pl.BlockSpec(memory_space=pl.ANY)] * 2,
        out_specs=(vmem, vmem),
        scratch_shapes=[
            pltpu.VMEM(meta_shape, F32),
            pltpu.VMEM((n_dp,) + meta_shape, F32),
            pltpu.VMEM((data, rhs), BF16),
            pltpu.VMEM((ka + 2 * kf, window * COLS), BF16),
            pltpu.VMEM((comps, data, ka), BF16),
            pltpu.VMEM((comps, data, 2 * kf), BF16),
            pltpu.VMEM((data, window * COLS), BF16),
            pltpu.VMEM((window * COLS, own * COLS), BF16),
            pltpu.VMEM((data, own * COLS), BF16),
            pltpu.VMEM((n_dp - 1, rows_here, rhs), BF16),
            pltpu.VMEM((n_dp, rows_here, rhs), BF16),
            pltpu.VMEM((rows_here, rhs), BF16),
            pltpu.VMEM((n_mp, chunk, rhs), BF16),
            dma((2, window)), dma((2, window)), dma((2, window)),
            dma((n_dp,)), dma((n_dp,)), dma((n_dp,)), dma((n_dp,)),
            dma((n_dp,)), dma((n_dp,)),
            dma((chunks,)), dma((n_mp,)),
            dma((n_mp,)), dma((chunks,)),
            dma((n_dp, chunks)), dma((n_dp, chunks)),
        ],
        compiler_params=pltpu.CompilerParams(
            collective_id=0, has_side_effects=True, vmem_limit_bytes=44 * 1024 * 1024
        ),
    )(
        data_rec[None], data_freq[None], data_coef.T, residual_cols,
        adjoint, forward.reshape(kf, cells),
    )
    return pl.pallas_call(
        functools.partial(finish, n_dp),
        out_shape=(
            jax.ShapeDtypeStruct((rows_here, rhs), BF16),
            jax.ShapeDtypeStruct((own * COLS, rhs), F32),
        ),
        in_specs=[vmem, vmem],
        out_specs=(vmem, vmem),
        compiler_params=pltpu.CompilerParams(vmem_limit_bytes=16 * 1024 * 1024),
    )(smooth_t, du_all)


def solution(mesh):
    in_specs = (
        P(None, None, "mp"),
        P(None, None, "mp"),
        P("dp"),
        P("dp"),
        P("dp", None),
        P("dp", None),
    )
    out_specs = (P("dp", None), P(("mp", "dp"), None))
    body = functools.partial(per_device, mesh.shape["mp"], mesh.shape["dp"])
    return jax.shard_map(body, mesh=mesh, in_specs=in_specs, out_specs=out_specs, check_vma=False)
```
